512 devices in a mesh: seq: 64 (over x, z), tp: 8 (over y, core).
Axes of the slice: x: 4, y: 4, z: 16, core: 2. Of those that a mesh axis runs over, the one named last changes fastest.
Arguments:
- queries: bfloat16 [16384, 4096], P('seq', 'tp'), may hold values from -122 to 122
- suffix_k: bfloat16 [16384, 1024], P('seq', 'tp'), may hold values from -6 to 6
- suffix_v: bfloat16 [16384, 1024], P('seq', 'tp'), may hold values from -6 to 6
- prefix_k: bfloat16 [8192, 1024], P('seq', 'tp'), may hold values from -8 to 8
- prefix_v: bfloat16 [8192, 1024], P('seq', 'tp'), may hold values from -6 to 6
- prefix_block: int32 [64], P('seq'), may hold values from 0 to 63, each once
- request_ids: int32 [64, 256], P('seq'), may hold values from 0 to 7, never falling along the last dimension, each value on 1 to 64 neighbouring positions
- out_weight: bfloat16 [4096, 4096], P('tp', 'seq'), may hold values from -0.09375 to 0.09375
Outputs:
- mixed: bfloat16 [16384, 4096], P('seq', 'tp')
The draws below stay inside these ranges and needn't reach their ends.
Inputs may be any that keep to these rules, and one draw needn't show every extreme that they name: `request_ids`: each row packs 8 requests in order, each of 1 to 64 slots, one of exactly 64. `prefix_block`: each prefix block appears once.
All inputs are finite; a program needn't handle non-finite values.
Results may differ from the reference program's by a relative error of at most 0.019.
Values may be sent and summed in bfloat16 or wider, within the bound.
A program may use at most 128 MiB of HBM per device.

```python
import math
import jax
import jax.numpy as jnp
import numpy as np
from jax import lax

D = 4096
QH = 32
KVH = 8
HD = 128
S_DEV = 256
PB_DEV = 128
REQ_DEV = 8
MOSTLEN = 64
SINKS = 4
TOKENS = 16384
PREFIX = 8192
WINDOW = 4096
N_SEQ = 64


def shared_keys(key):
    base = jnp.clip(jax.random.normal(jax.random.fold_in(key, 11), (PREFIX, KVH * HD), jnp.float32), -6.0, 6.0)
    return base


def draw_prefix_k(key, part):
    return shared_keys(key).astype(jnp.bfloat16)


def draw_queries(key, part):
    base = jnp.clip(jax.random.normal(jax.random.fold_in(key, 12), (TOKENS, QH * HD), jnp.float32), -6.0, 6.0)
    return base.astype(jnp.bfloat16)


def levels(own_key, extent, shards, least, high):
    def one(axis_at, blocks):
        draws = jax.random.uniform(jax.random.fold_in(jax.random.fold_in(own_key, 6), axis_at), (blocks,), jnp.float32, least / len(shards), high / len(shards))
        return jnp.repeat(jnp.exp(draws), extent[axis_at] // blocks).reshape((-1,) + (1,) * (len(extent) - axis_at - 1))

    factor_of = one(*shards[0])
    for cut in shards[1:]:
        factor_of = factor_of * one(*cut)
    return factor_of


def profile(count, total, bound, slope):
    loads = [(1 << 20) // math.isqrt(rank ** slope) + 1 for rank in range(2, count + 1)]
    surplus, counts = total - bound - (count - 1), [1] * (count - 1)
    while surplus > 0:
        free = [i for i in range(count - 1) if counts[i] < bound]
        whole, left = sum([loads[i] for i in free]), surplus
        for i in free:
            extra = min(bound - counts[i], max(1, left * loads[i] // whole), surplus)
            counts[i] = counts[i] + extra
            surplus = surplus - extra
    return np.array([bound] + counts)


def ragged(key, amount, total, reach, skew):
    if amount == 2:
        one = jax.random.randint(key, (), max(1, total - reach), min(reach, total - 1) + 1)
        return jnp.stack([one, total - one])
    lengths = jnp.asarray(profile(amount, total, reach, skew), jnp.int32)
    couples = (amount - 1) // 2
    source_of, receiver = lengths[1:1 + 2 * couples:2], lengths[2:2 + 2 * couples:2]
    margin = jnp.minimum(source_of - 1, reach - receiver)
    shifted = jax.random.randint(jax.random.fold_in(key, 1), (couples,), 0, 1 << 20) % (margin + 1)
    lengths = lengths.at[1:1 + 2 * couples:2].set(source_of - shifted).at[2:2 + 2 * couples:2].set(receiver + shifted)
    return lengths[jax.random.permutation(jax.random.fold_in(key, 2), amount)]


def scatter_about(own_key, dims, deviation, most, cuts=(), kind=jnp.bfloat16):
    factor_of = levels(own_key, dims, cuts, -0.22, 0.18) if cuts else 1.0
    array = jax.random.normal(own_key, dims, jnp.float32) * deviation * factor_of
    return jnp.minimum(jnp.maximum(array, -most), most).astype(kind)


def setup_inputs(seed: int = 0) -> dict:
    key_list = jax.random.split(jax.random.key(seed), 9)
    queries = draw_queries(jax.random.fold_in(key_list[8], 71), 0)
    suffix_k = scatter_about(key_list[1], (TOKENS, KVH * HD), 1.0, 6.0, ((0, 64), (1, 8)))
    suffix_v = scatter_about(key_list[2], (TOKENS, KVH * HD), 1.0, 6.0, ((0, 64), (1, 8)))
    prefix_k = draw_prefix_k(jax.random.fold_in(key_list[8], 71), 0)
    prefix_v = scatter_about(key_list[4], (PREFIX, KVH * HD), 1.0, 6.0, ((0, 64), (1, 8)))
    prefix_block = jax.random.permutation(key_list[5], N_SEQ).astype(jnp.int32)
    request_ids = jax.vmap(lambda own: jnp.searchsorted(jnp.cumsum(ragged(own, REQ_DEV, S_DEV, MOSTLEN, 2)), jnp.arange(S_DEV), side="right"))(jax.random.split(key_list[6], N_SEQ)).reshape((N_SEQ, S_DEV)).astype(jnp.int32)
    out_weight = scatter_about(key_list[7], (QH * HD, D), (QH * HD) ** -0.5, 0.09375, ((0, 8), (1, 64)))
    return dict(queries=queries, suffix_k=suffix_k, suffix_v=suffix_v, prefix_k=prefix_k, prefix_v=prefix_v, prefix_block=prefix_block, request_ids=request_ids, out_weight=out_weight)


def attend_block(query_block, key_block, value_block, request, prefix_k, prefix_v, prefix_pos):
    count = request.shape[0]
    slots = jnp.arange(count, dtype=jnp.int32)
    same = request[:, None] == request[None, :]
    offsets = lax.optimization_barrier(jnp.sum((same & (slots[None, :] < slots[:, None])).astype(jnp.int32), axis=1))
    query_pos = PREFIX + offsets
    prefix_mask = (prefix_pos[None, :] >= query_pos[:, None] - WINDOW + 1) | (prefix_pos[None, :] < SINKS)
    own_mask = same & (slots[None, :] <= slots[:, None])
    allowed = jnp.concatenate([prefix_mask, own_mask], axis=1)
    keys = jnp.concatenate([prefix_k, key_block], axis=0).astype(jnp.float32).reshape(-1, KVH, HD)
    values = jnp.concatenate([prefix_v, value_block], axis=0).astype(jnp.float32).reshape(-1, KVH, HD)
    grouped = query_block.astype(jnp.float32).reshape(count, KVH, QH // KVH, HD)
    scores = jnp.einsum('shgd,nhd->hgsn', grouped, keys, precision=lax.Precision.HIGHEST) / math.sqrt(HD)
    scores = jnp.where(allowed, scores, jnp.float32(-1e+30))
    top = lax.optimization_barrier(jnp.max(scores, axis=-1, keepdims=True))
    weights = jnp.where(allowed, jnp.exp(scores - top), jnp.float32(0.0))
    total = lax.optimization_barrier(jnp.sum(weights, axis=-1))
    rounded = lax.optimization_barrier(weights.astype(jnp.bfloat16)).astype(jnp.float32)
    summed = jnp.einsum('hgsn,nhd->hgsd', rounded, values, precision=lax.Precision.HIGHEST)
    attended = summed / total[..., None]
    return attended.transpose(2, 0, 1, 3).reshape(count, QH * HD).astype(jnp.bfloat16)

def reference(queries, suffix_k, suffix_v, prefix_k, prefix_v, prefix_block, request_ids, out_weight):
    prefix_pos = (prefix_block[:, None] * PB_DEV + jnp.arange(PB_DEV, dtype=jnp.int32)[None, :]).reshape(PREFIX).astype(jnp.int32)
    query_blocks = queries.reshape(N_SEQ, S_DEV, QH * HD)
    key_blocks = suffix_k.reshape(N_SEQ, S_DEV, KVH * HD)
    value_blocks = suffix_v.reshape(N_SEQ, S_DEV, KVH * HD)

    def one_block(items):
        return attend_block(items[0], items[1], items[2], items[3], prefix_k, prefix_v, prefix_pos)
    attended = lax.map(one_block, (query_blocks, key_blocks, value_blocks, request_ids))
    attended = attended.reshape(TOKENS, QH * HD)
    return jnp.dot(attended, out_weight, preferred_element_type=jnp.float32).astype(jnp.bfloat16)
```

```python
import functools
import math

import jax
import jax.numpy as jnp
from jax import lax
from jax.experimental import pallas as pl
from jax.experimental.pallas import tpu as pltpu
from jax.sharding import PartitionSpec as P

HD = 128
SINKS = 4
NX = 4
MESH = pl.DeviceIdType.MESH
LOG2E = 1.4426950408889634


def gather_kernel(nz, a_ref, b_ref, i_ref, ga, gb, gi, sa, sb, si, ra_x, rb_z, ra_z, ri_x, ri_z, rb_x, own):
    half = nz // 2
    rows_b = b_ref.shape[0]
    low = rows_b // 2
    me = lax.axis_index("seq")
    x, z = me // nz, lax.rem(me, nz)
    count = NX * nz

    def slot(dx, dz):
        return lax.rem(x + dx + NX, NX) * nz + lax.rem(z + dz + nz, nz)

    def dev(dx, dz):
        return {"seq": slot(dx, dz)}

    right, left, up, down = dev(1, 0), dev(-1, 0), dev(0, 1), dev(0, -1)
    barrier = pltpu.get_barrier_semaphore()
    for peer in (right, left, dev(2, 0), up, down):
        pl.semaphore_signal(barrier, inc=1, device_id=peer, device_id_type=MESH)
    pl.semaphore_wait(barrier, 5)

    def push(src, dst, ssem, rsem, to):
        pltpu.make_async_remote_copy(
            src_ref=src, dst_ref=dst, send_sem=ssem, recv_sem=rsem, device_id=to, device_id_type=MESH
        ).start()

    def arrived(ref, sem):
        pltpu.make_async_copy(ref, ref, sem).wait()

    keep = [
        pltpu.make_async_copy(a_ref, ga.at[me], own.at[0]),
        pltpu.make_async_copy(b_ref, gb.at[me], own.at[1]),
        pltpu.make_async_copy(i_ref, gi.at[me], own.at[2]),
    ]

    def a_move(dx, dist, way):
        at = slot(dx, -way * dist)
        src = a_ref if (dx == 0 and dist == 0) else ga.at[at]
        sem = ra_z.at[dx, 0 if way > 0 else 1, dist]
        push(src, ga.at[at], sa, sem, up if way > 0 else down)

    def i_move(dx, dist, way):
        at = slot(dx, -way * dist)
        src = i_ref if (dx == 0 and dist == 0) else gi.at[at]
        sem = ri_z.at[dx, 0 if way > 0 else 1, dist]
        push(src, gi.at[at], si, sem, up if way > 0 else down)

    def b_move(dist, way):
        at = slot(0, -way * dist)
        src = b_ref if dist == 0 else gb.at[at]
        push(src, gb.at[at], sb, rb_z.at[0 if way > 0 else 1, dist], up if way > 0 else down)

    def b_side(dist, way):
        at = slot(0, -way * dist)
        src = b_ref if dist == 0 else gb.at[at]
        lane = 0 if way > 0 else 1
        push(src, gb.at[at], sb, rb_x.at[0, lane, dist], right)
        push(src, gb.at[at], sb, rb_x.at[1, lane, dist], left)

    def b_relay(dist, way):
        lane = 0 if way > 0 else 1
        at = slot(-1, -way * dist)
        arrived(gb.at[at], rb_x.at[0, lane, dist])
        push(gb.at[at, pl.ds(0, low)], gb.at[at, pl.ds(0, low)], sb, rb_x.at[2, lane, dist], right)
        at = slot(1, -way * dist)
        arrived(gb.at[at], rb_x.at[1, lane, dist])
        rest = pl.ds(low, rows_b - low)
        push(gb.at[at, rest], gb.at[at, rest], sb, rb_x.at[3, lane, dist], left)

    for dx in (1, 3, 2):
        push(a_ref, ga.at[me], sa, ra_x.at[dx], dev(dx, 0))
        push(i_ref, gi.at[me], si, ri_x.at[dx], dev(dx, 0))
    b_move(0, 1)
    b_move(0, -1)
    b_side(0, 1)
    a_move(0, 0, 1)
    a_move(0, 0, -1)
    i_move(0, 0, 1)
    i_move(0, 0, -1)
    for copy in keep:
        copy.start()
    for dx in (1, 3, 2):
        arrived(ga.at[slot(dx, 0)], ra_x.at[NX - dx])
        a_move(dx, 0, 1)
        a_move(dx, 0, -1)
        arrived(gi.at[slot(dx, 0)], ri_x.at[NX - dx])
        i_move(dx, 0, 1)
        i_move(dx, 0, -1)
    for k in range(1, half + 1):
        for way in (1, -1):
            last = half if way > 0 else half - 1
            lane = 0 if way > 0 else 1
            if k <= last:
                arrived(gb.at[slot(0, -way * k)], rb_z.at[lane, k - 1])
                if k < last:
                    b_move(k, way)
                b_side(k, way)
        for dx in (0, 1, 3, 2):
            for way in (1, -1):
                last = half if way > 0 else half - 1
                lane = 0 if way > 0 else 1
                if k <= last:
                    arrived(ga.at[slot(dx, -way * k)], ra_z.at[dx, lane, k - 1])
                    if k < last:
                        a_move(dx, k, way)
                    arrived(gi.at[slot(dx, -way * k)], ri_z.at[dx, lane, k - 1])
                    if k < last:
                        i_move(dx, k, way)
        for way in (1, -1):
            if k - 1 == 0 and way < 0:
                continue
            b_relay(k - 1, way)
    b_relay(half, 1)
    for dist in range(half + 1):
        for way in (1, -1):
            if way < 0 and (dist == 0 or dist == half):
                continue
            lane = 0 if way > 0 else 1
            at = slot(2, -way * dist)
            arrived(gb.at[at, pl.ds(0, low)], rb_x.at[2, lane, dist])
            arrived(gb.at[at, pl.ds(low, rows_b - low)], rb_x.at[3, lane, dist])
    for copy in keep:
        copy.wait()
    arrived(ga.at[pl.ds(0, count - 1)], sa)
    arrived(gb.at[pl.ds(0, count - 1)], sb)
    arrived(gi.at[pl.ds(0, count - 1)], si)


def gather(nz, pa, pb, ids):
    count = NX * nz
    half = nz // 2
    anywhere = pl.BlockSpec(memory_space=pl.ANY)
    dma = pltpu.SemaphoreType.DMA
    return pl.pallas_call(
        functools.partial(gather_kernel, nz),
        out_shape=(
            jax.ShapeDtypeStruct((count,) + pa.shape, pa.dtype),
            jax.ShapeDtypeStruct((count,) + pb.shape, pb.dtype),
            jax.ShapeDtypeStruct((count,) + ids.shape, ids.dtype),
        ),
        in_specs=[anywhere] * 3,
        out_specs=(anywhere,) * 3,
        scratch_shapes=[
            dma, dma, dma,
            dma((NX,)),
            dma((2, half)),
            dma((NX, 2, half)),
            dma((NX,)),
            dma((NX, 2, half)),
            dma((4, 2, half + 1)),
            dma((3,)),
        ],
        compiler_params=pltpu.CompilerParams(collective_id=0, has_side_effects=True),
        name="gather",
    )(pa, pb, ids)


def attend_kernel(q_ref, sk_ref, sv_ref, row_ref, col_ref, gi, ga, gb, out_ref,
                  ks, vs, scores, att, inv_v, inv_s, sem):
    count = ga.shape[0]
    first = count // 2
    tokens = q_ref.shape[0]
    heads = q_ref.shape[1] // HD
    main = first * HD
    total = main + HD + tokens
    tile = 512
    lane = lax.broadcasted_iota(jnp.int32, (1, HD), 1)
    which = lax.broadcasted_iota(jnp.int32, (count, 1, HD), 0)
    inv_v[...] = jnp.sum(jnp.where(gi[...] == lane[None], which, 0), axis=0)
    copy = pltpu.make_async_copy(inv_v, inv_s, sem)
    copy.start()
    copy.wait()

    def fill(i, _):
        at = inv_s[0, first + i]
        to = pl.multiple_of(i * HD, HD)
        ks[pl.ds(to, HD), :] = ga[at, :HD, :]
        vs[pl.ds(to, HD), :] = gb[at, :HD, :]
        return 0

    lax.fori_loop(0, first, fill, 0)
    at = inv_s[0, 0]
    ks[main:main + HD, :] = ga[at, :HD, :]
    vs[main:main + HD, :] = gb[at, :HD, :]
    ks[main + HD:, :] = sk_ref[...]
    vs[main + HD:, :] = sv_ref[...]

    same = col_ref[...] == row_ref[...]
    mine = lax.broadcasted_iota(jnp.int32, (tokens, tokens), 0)
    other = lax.broadcasted_iota(jnp.int32, (tokens, tokens), 1)
    offset = jnp.sum(jnp.where(same & (other < mine), 1.0, 0.0), axis=1, keepdims=True)
    lane_f = lane.astype(jnp.float32)
    edge = lane_f > offset
    own = same & (other <= mine)
    sink = lane < SINKS
    low = jnp.float32(-1e30)
    gain = jnp.float32(LOG2E / math.sqrt(HD))
    bounds = [(t, min(tile, total - t)) for t in range(0, main, tile)] + [(main, total - main)]

    def nt(a, b):
        return lax.dot_general(a, b, (((1,), (1,)), ((), ())), preferred_element_type=jnp.float32)

    for h in range(heads):
        q = q_ref[:, h * HD:(h + 1) * HD]
        top = jnp.full((tokens, HD), low, jnp.float32)
        for start, size in bounds:
            s = nt(q, ks[start:start + size, :])
            parts = [s[:, j:j + HD] for j in range(0, size, HD)]
            if start == 0:
                parts[0] = jnp.where(edge, parts[0], low)
            if start == main:
                parts[0] = jnp.where(sink, parts[0], low)
                for j in range(1, len(parts)):
                    parts[j] = jnp.where(own[:, (j - 1) * HD:j * HD], parts[j], low)
            for j, part in enumerate(parts):
                scores[:, start + j * HD:start + (j + 1) * HD] = part
                top = jnp.maximum(top, part)
        top = jnp.max(top, axis=1, keepdims=True)
        sums = jnp.zeros((tokens, HD), jnp.float32)
        acc = jnp.zeros((tokens, HD), jnp.float32)
        for start, size in bounds:
            w = jnp.exp2((scores[:, start:start + size] - top) * gain)
            for j in range(0, size, HD):
                sums = sums + w[:, j:j + HD]
            acc = acc + jnp.dot(w.astype(jnp.bfloat16), vs[start:start + size, :],
                                preferred_element_type=jnp.float32)
        att[:, h * HD:(h + 1) * HD] = (acc / jnp.sum(sums, axis=1, keepdims=True)).astype(jnp.bfloat16)

    cols = (ga.shape[1] - HD)
    group = tile // cols

    def project(g, _):
        pieces = []
        for h in range(heads):
            if h == 0:
                part = ga[pl.ds(g * group, group), HD:, :]
            else:
                part = gb[pl.ds(g * group, group), HD + (h - 1) * cols:HD + h * cols, :]
            pieces.append(part.reshape(group * cols, HD))
        w = jnp.concatenate(pieces, axis=1)
        to = pl.multiple_of(g * tile, tile)
        out_ref[:, pl.ds(to, tile)] = nt(att[...], w).astype(jnp.bfloat16)
        return 0

    lax.fori_loop(0, count // group, project, 0)


def attend(queries, suffix_k, suffix_v, row, col, gi, ga, gb):
    count = ga.shape[0]
    tokens = queries.shape[0]
    total = count // 2 * HD + HD + tokens
    width = count * (ga.shape[1] - HD)
    return pl.pallas_call(
        attend_kernel,
        out_shape=jax.ShapeDtypeStruct((tokens, width), jnp.bfloat16),
        scratch_shapes=[
            pltpu.VMEM((total, HD), jnp.bfloat16),
            pltpu.VMEM((total, HD), jnp.bfloat16),
            pltpu.VMEM((tokens, total), jnp.float32),
            pltpu.VMEM((tokens, queries.shape[1]), jnp.bfloat16),
            pltpu.VMEM((1, HD), jnp.int32),
            pltpu.SMEM((1, HD), jnp.int32),
            pltpu.SemaphoreType.DMA,
        ],
        compiler_params=pltpu.CompilerParams(vmem_limit_bytes=56 * 2**20),
        name="attend",
    )(queries, suffix_k, suffix_v, row, col, gi, ga, gb)


def local(queries, suffix_k, suffix_v, prefix_k, prefix_v, prefix_block, request_ids, out_weight):
    nz = lax.axis_size("seq") // NX
    cols = out_weight.shape[1]
    heads = out_weight.shape[0] // HD
    flipped = out_weight.T
    pieces = [flipped[:, h * HD:(h + 1) * HD] for h in range(heads)]
    pa = jnp.concatenate([prefix_k] + pieces[:1], axis=0)
    pb = jnp.concatenate([prefix_v] + pieces[1:], axis=0)
    ids = jnp.broadcast_to(prefix_block[:, None], (1, HD))
    ga, gb, gi = gather(nz, pa, pb, ids)
    col = request_ids.reshape(-1, 1)
    partial_out = attend(queries, suffix_k, suffix_v, request_ids, col, gi, ga, gb)
    return lax.psum_scatter(partial_out, "tp", scatter_dimension=1, tiled=True)


def solution(mesh):
    placed = (
        P("seq", "tp"),
        P("seq", "tp"),
        P("seq", "tp"),
        P("seq", "tp"),
        P("seq", "tp"),
        P("seq"),
        P("seq", None),
        P("tp", "seq"),
    )
    return jax.shard_map(
        local, mesh=mesh, in_specs=placed, out_specs=P("seq", "tp"), check_vma=False
    )
```

```python
import functools
import math

import jax
import jax.numpy as jnp
from jax import lax
from jax.experimental import pallas as pl
from jax.experimental.pallas import tpu as pltpu
from jax.sharding import PartitionSpec as P

HD = 128
SINKS = 4
NX = 4
NY = 4
PART = 96
MESH = pl.DeviceIdType.MESH
LOG2E = 1.4426950408889634


def push(src, dst, ssem, rsem, to):
    pltpu.make_async_remote_copy(
        src_ref=src, dst_ref=dst, send_sem=ssem, recv_sem=rsem, device_id=to, device_id_type=MESH
    ).start()


def arrived(ref, sem):
    pltpu.make_async_copy(ref, ref, sem).wait()


def nt(a, b):
    return lax.dot_general(a, b, (((1,), (1,)), ((), ())), preferred_element_type=jnp.float32)


class Rings:
    def __init__(self, nz, x, z, ga, gb, sems, gi=None, isems=None):
        self.nz, self.x, self.z, self.half = nz, x, z, nz // 2
        self.ga, self.gb, self.gi = ga, gb, gi
        self.sa, self.sb, self.ra_x, self.rb_z, self.ra_z, self.rb_x = sems
        if gi is not None:
            self.si, self.ri_x, self.ri_z = isems
        self.rows_b = gb.shape[1]
        self.low = self.rows_b // 2
        self.right, self.left = self.dev(1, 0), self.dev(-1, 0)
        self.ends = {1: self.dev(0, 1), -1: self.dev(0, -1)}

    def slot(self, dx, dz):
        return lax.rem(self.x + dx + NX, NX) * self.nz + lax.rem(self.z + dz + self.nz, self.nz)

    def dev(self, dx, dz):
        return {"seq": self.slot(dx, dz)}

    def last(self, way):
        return self.half if way > 0 else self.half - 1

    def a_move(self, dx, dist, way):
        at = self.slot(dx, -way * dist)
        lane = 0 if way > 0 else 1
        push(self.ga.at[at], self.ga.at[at], self.sa, self.ra_z.at[dx, lane, dist], self.ends[way])
        if self.gi is not None:
            push(self.gi.at[at], self.gi.at[at], self.si, self.ri_z.at[dx, lane, dist], self.ends[way])

    def a_wait(self, dx, dist, way):
        at = self.slot(dx, -way * dist)
        lane = 0 if way > 0 else 1
        arrived(self.ga.at[at], self.ra_z.at[dx, lane, dist - 1])
        if self.gi is not None:
            arrived(self.gi.at[at], self.ri_z.at[dx, lane, dist - 1])

    def b_move(self, dist, way):
        at = self.slot(0, -way * dist)
        push(self.gb.at[at], self.gb.at[at], self.sb, self.rb_z.at[0 if way > 0 else 1, dist], self.ends[way])

    def b_side(self, dist, way):
        at = self.slot(0, -way * dist)
        lane = 0 if way > 0 else 1
        push(self.gb.at[at], self.gb.at[at], self.sb, self.rb_x.at[0, lane, dist], self.right)
        push(self.gb.at[at], self.gb.at[at], self.sb, self.rb_x.at[1, lane, dist], self.left)

    def halves(self, at):
        return self.gb.at[at, pl.ds(0, self.low)], self.gb.at[at, pl.ds(self.low, self.rows_b - self.low)]

    def b_relay(self, dist, way):
        lane = 0 if way > 0 else 1
        at = self.slot(-1, -way * dist)
        arrived(self.gb.at[at], self.rb_x.at[0, lane, dist])
        part = self.halves(at)[0]
        push(part, part, self.sb, self.rb_x.at[2, lane, dist], self.right)
        at = self.slot(1, -way * dist)
        arrived(self.gb.at[at], self.rb_x.at[1, lane, dist])
        part = self.halves(at)[1]
        push(part, part, self.sb, self.rb_x.at[3, lane, dist], self.left)

    def begin(self):
        me = self.slot(0, 0)
        for dx in (1, 3, 2):
            push(self.ga.at[me], self.ga.at[me], self.sa, self.ra_x.at[dx], self.dev(dx, 0))
            if self.gi is not None:
                push(self.gi.at[me], self.gi.at[me], self.si, self.ri_x.at[dx], self.dev(dx, 0))
        self.b_move(0, 1)
        self.b_move(0, -1)
        self.b_side(0, 1)
        self.a_move(0, 0, 1)
        self.a_move(0, 0, -1)

    def spread(self):
        for dx in (1, 3, 2):
            arrived(self.ga.at[self.slot(dx, 0)], self.ra_x.at[NX - dx])
            if self.gi is not None:
                arrived(self.gi.at[self.slot(dx, 0)], self.ri_x.at[NX - dx])
            self.a_move(dx, 0, 1)
            self.a_move(dx, 0, -1)

    def step(self, k):
        for way in (1, -1):
            if k <= self.last(way):
                arrived(self.gb.at[self.slot(0, -way * k)], self.rb_z.at[0 if way > 0 else 1, k - 1])
                if k < self.last(way):
                    self.b_move(k, way)
                self.b_side(k, way)
        for dx in (0, 1, 3, 2):
            for way in (1, -1):
                if k <= self.last(way):
                    self.a_wait(dx, k, way)
                    if k < self.last(way):
                        self.a_move(dx, k, way)
        for way in (1, -1):
            if k - 1 > 0 or way > 0:
                self.b_relay(k - 1, way)

    def finish(self):
        self.b_relay(self.half, 1)
        for dist in range(self.half + 1):
            for way in (1, -1):
                if way < 0 and (dist == 0 or dist == self.half):
                    continue
                lane = 0 if way > 0 else 1
                low, high = self.halves(self.slot(2, -way * dist))
                arrived(low, self.rb_x.at[2, lane, dist])
                arrived(high, self.rb_x.at[3, lane, dist])

    def drain(self):
        count = NX * self.nz
        arrived(self.ga.at[pl.ds(0, count - 1)], self.sa)
        arrived(self.gb.at[pl.ds(0, count - 1)], self.sb)
        if self.gi is not None:
            arrived(self.gi.at[pl.ds(0, count - 1)], self.si)


def kernel(nz, q_ref, sk_ref, sv_ref, pk_ref, pv_ref, block_ref, row_ref, w_ref, out_ref,
           ga, gb, gi, wa, wb, wt, ks, vs, scores, att, inv_v, inv_s, sem, *sems):
    ring_sems, id_sems, w_sems = sems[0:6], sems[6:9], sems[9:15]
    sp, rp, sg, rg_y, rg_c = sems[15:]
    half = nz // 2
    count = NX * nz
    first = count // 2
    tokens = q_ref.shape[0]
    heads = q_ref.shape[1] // HD
    cols = w_ref.shape[1]
    me, t = lax.axis_index("seq"), lax.axis_index("tp")
    x, z, y, c = me // nz, lax.rem(me, nz), t // 2, lax.rem(t, 2)

    other_half = z // half
    w_slot = lax.rem(y + 1, NX) * nz + lax.rem(half * other_half + 2 * lax.rem(z, half) + c - nz // 4 + nz, nz)
    w_to = {"seq": w_slot, "tp": 2 * x + other_half}
    v = lax.rem(z + nz // 4 - half * c + nz, nz)
    w_from = {"seq": y * nz + half * c + v // 2, "tp": 2 * lax.rem(x + NX - 1, NX) + lax.rem(v, 2)}
    partner = {"tp": 2 * y + 1 - c}

    def column(dy):
        return 2 * lax.rem(y + dy, NY) + c

    kv = Rings(nz, x, z, ga, gb, ring_sems, gi, id_sems)
    wr = Rings(nz, x, z, wa, wb, w_sems)

    barrier = pltpu.get_barrier_semaphore()
    peers = [kv.dev(1, 0), kv.dev(-1, 0), kv.dev(2, 0), kv.dev(0, 1), kv.dev(0, -1), w_to, w_from, partner]
    peers = peers + [{"tp": column(dy)} for dy in range(1, NY)]
    for peer in peers:
        pl.semaphore_signal(barrier, inc=1, device_id=peer, device_id_type=MESH)

    ga[me] = pk_ref[:PART, :]
    gb[me, :HD, :] = pv_ref[...]
    gb[me, HD:, :] = pk_ref[PART:, :]
    gi[me] = jnp.full((1, HD), block_ref[0], jnp.int32)
    flipped = w_ref[...].astype(jnp.float32).T.astype(jnp.bfloat16)
    for h in range(heads):
        wt[h * cols:(h + 1) * cols, :] = flipped[:, h * HD:(h + 1) * HD]

    row = jnp.broadcast_to(row_ref[...].astype(jnp.float32), (tokens, tokens))
    col = row.T
    mine = lax.broadcasted_iota(jnp.int32, (tokens, tokens), 0)
    other = lax.broadcasted_iota(jnp.int32, (tokens, tokens), 1)
    same = jnp.where(row == col, 1.0, 0.0)
    offset = jnp.sum(jnp.where(other < mine, same, 0.0), axis=1, keepdims=True)
    lane = lax.broadcasted_iota(jnp.int32, (1, HD), 1)
    low = jnp.float32(-1e30)
    main = first * HD
    total = main + HD + tokens
    ks[main + HD:, :] = sk_ref[...]
    vs[main + HD:, :] = sv_ref[...]

    pl.semaphore_wait(barrier, len(peers))
    kv.begin()
    push(wt.at[pl.ds(0, PART)], wa.at[w_slot], sp, rp.at[0], w_to)
    push(wt.at[pl.ds(PART, wt.shape[0] - PART)], wb.at[w_slot], sp, rp.at[1], w_to)
    kv.spread()
    for k in range(1, half + 1):
        kv.step(k)
        if k == max(half - 1, 1):
            arrived(wa.at[me], rp.at[0])
            arrived(wb.at[me], rp.at[1])
            wr.begin()
    kv.finish()
    wr.spread()

    which = lax.broadcasted_iota(jnp.int32, (count, 1, HD), 0)
    inv_v[...] = jnp.max(jnp.where(gi[...] == lane[None], which, 0), axis=0)
    copy = pltpu.make_async_copy(inv_v, inv_s, sem)
    copy.start()
    copy.wait()

    def fetch(to, at):
        ks[pl.ds(to, PART), :] = ga[at]
        ks[pl.ds(to + PART, HD - PART), :] = gb[at, HD:, :]
        vs[pl.ds(to, HD), :] = gb[at, :HD, :]

    def fill(i, _):
        fetch(pl.multiple_of(i * HD, HD), inv_s[0, first + i])
        return 0

    lax.fori_loop(0, first, fill, 0)
    fetch(main, inv_s[0, 0])

    edge = lane.astype(jnp.float32) > offset
    own = (same > 0.5) & (other <= mine)
    sink = lane < SINKS
    gain = jnp.float32(LOG2E / math.sqrt(HD))
    tile = 512
    bounds = [(s, min(tile, total - s)) for s in range(0, main, tile)] + [(main, total - main)]

    def ag_send(h):
        at = t * heads + h
        for dy in (1, 3, 2):
            push(att.at[at], att.at[at], sg, rg_y.at[dy, h], {"tp": column(dy)})
        push(att.at[at], att.at[at], sg, rg_c.at[0, h], partner)

    def ag_relay(h):
        for dy in (1, 3, 2):
            at = column(dy) * heads + h
            arrived(att.at[at], rg_y.at[NY - dy, h])
            push(att.at[at], att.at[at], sg, rg_c.at[dy, h], partner)

    ticks = iter(range(1, half + 1))

    def tick():
        k = next(ticks, None)
        if k is not None:
            wr.step(k)

    for h in range(heads):
        q = q_ref[:, h * HD:(h + 1) * HD]
        top = jnp.full((tokens, HD), low, jnp.float32)
        for start, size in bounds:
            s = nt(q, ks[start:start + size, :])
            parts = [s[:, j:j + HD] for j in range(0, size, HD)]
            if start == 0:
                parts[0] = jnp.where(edge, parts[0], low)
            if start == main:
                parts[0] = jnp.where(sink, parts[0], low)
                for j in range(1, len(parts)):
                    parts[j] = jnp.where(own[:, (j - 1) * HD:j * HD], parts[j], low)
            for j, part in enumerate(parts):
                scores[:, start + j * HD:start + (j + 1) * HD] = part
                top = jnp.maximum(top, part)
        top = jnp.max(top, axis=1, keepdims=True)
        tick()
        sums = jnp.zeros((tokens, HD), jnp.float32)
        acc = jnp.zeros((tokens, HD), jnp.float32)
        for start, size in bounds:
            w = jnp.exp2((scores[:, start:start + size] - top) * gain)
            for j in range(0, size, HD):
                sums = sums + w[:, j:j + HD]
            acc = acc + jnp.dot(w.astype(jnp.bfloat16), vs[start:start + size, :],
                                preferred_element_type=jnp.float32)
        att[t * heads + h] = (acc / jnp.sum(sums, axis=1, keepdims=True)).astype(jnp.bfloat16)
        tick()
        ag_send(h)
        if h > 0:
            ag_relay(h - 1)
    ag_relay(heads - 1)
    for k in ticks:
        wr.step(k)
    wr.finish()
    for dy in range(NY):
        for h in range(heads):
            at = (2 * lax.rem(y + dy, NY) + 1 - c) * heads + h
            arrived(att.at[at], rg_c.at[dy, h])

    cut = PART - cols
    result = jnp.zeros((tokens, out_ref.shape[1]), jnp.float32)
    for yy in range(NY):
        for cc in range(2):
            base = ((yy + 1) % NX) * nz
            spots = [base + lax.rem(half * c - nz // 4 + cc + 2 * u + nz, nz) for u in range(half)]
            a = [wa[s] for s in spots]
            b = [wb[s] for s in spots]
            rest = cols - cut
            weight = [
                [p[:cols] for p in a],
                [piece for p, r in zip(a, b) for piece in (p[cols:], r[:rest])],
                [r[rest:rest + cols] for r in b],
                [r[rest + cols:] for r in b],
            ]
            w = jnp.concatenate([jnp.concatenate(pieces, axis=0) for pieces in weight], axis=1)
            from_t = (2 * yy + cc) * heads
            a = jnp.concatenate([att[from_t + h] for h in range(heads)], axis=1)
            result = result + nt(a, w)
    out_ref[...] = result.astype(out_ref.dtype)

    kv.drain()
    wr.drain()
    arrived(wt, sp)
    arrived(att.at[pl.ds(0, (NY - 1) * heads + NY * heads)], sg)


def local(queries, suffix_k, suffix_v, prefix_k, prefix_v, prefix_block, request_ids, out_weight):
    count = lax.axis_size("seq")
    nz = count // NX
    half = nz // 2
    tp = lax.axis_size("tp")
    tokens, width = queries.shape
    heads = width // HD
    cols = out_weight.shape[1]
    total = count // 2 * HD + HD + tokens
    bf = jnp.bfloat16
    dma = pltpu.SemaphoreType.DMA
    ring = [dma, dma, dma((NX,)), dma((2, half)), dma((NX, 2, half)), dma((4, 2, half + 1))]
    whole = pl.BlockSpec(memory_space=pltpu.VMEM)
    return pl.pallas_call(
        functools.partial(kernel, nz),
        out_shape=jax.ShapeDtypeStruct((tokens, cols * count // tp), bf),
        in_specs=[whole] * 5 + [pl.BlockSpec(memory_space=pltpu.SMEM)] + [whole] * 2,
        out_specs=whole,
        scratch_shapes=[
            pltpu.VMEM((count, PART, HD), bf),
            pltpu.VMEM((count, 2 * HD - PART, HD), bf),
            pltpu.VMEM((count, 1, HD), jnp.int32),
            pltpu.VMEM((count, PART, HD), bf),
            pltpu.VMEM((count, heads * cols - PART, HD), bf),
            pltpu.VMEM((heads * cols, HD), bf),
            pltpu.VMEM((total, HD), bf),
            pltpu.VMEM((total, HD), bf),
            pltpu.VMEM((tokens, total), jnp.float32),
            pltpu.VMEM((tp * heads, tokens, HD), bf),
            pltpu.VMEM((1, HD), jnp.int32),
            pltpu.SMEM((1, HD), jnp.int32),
            dma,
        ] + ring + [dma, dma((NX,)), dma((NX, 2, half))] + ring
        + [dma, dma((2,)), dma, dma((NY, heads)), dma((NY, heads))],
        compiler_params=pltpu.CompilerParams(
            collective_id=0, has_side_effects=True, vmem_limit_bytes=56 * 2**20
        ),
        name="block",
    )(queries, suffix_k, suffix_v, prefix_k, prefix_v, prefix_block, request_ids, out_weight)


def solution(mesh):
    placed = (
        P("seq", "tp"),
        P("seq", "tp"),
        P("seq", "tp"),
        P("seq", "tp"),
        P("seq", "tp"),
        P("seq"),
        P("seq", None),
        P("tp", "seq"),
    )
    return jax.shard_map(
        local, mesh=mesh, in_specs=placed, out_specs=P("seq", "tp"), check_vma=False
    )
```

```python
import functools
import math

import jax
import jax.numpy as jnp
from jax import lax
from jax.experimental import pallas as pl
from jax.experimental.pallas import tpu as pltpu
from jax.sharding import PartitionSpec as P

HD = 128
SINKS = 4
NX = 4
NY = 4
PART = 96
LEAD = 2
MESH = pl.DeviceIdType.MESH
LOG2E = 1.4426950408889634


def push(src, dst, ssem, rsem, to):
    pltpu.make_async_remote_copy(
        src_ref=src, dst_ref=dst, send_sem=ssem, recv_sem=rsem, device_id=to, device_id_type=MESH
    ).start()


def arrived(ref, sem):
    pltpu.make_async_copy(ref, ref, sem).wait()


def nt(a, b):
    return lax.dot_general(a, b, (((1,), (1,)), ((), ())), preferred_element_type=jnp.float32)


class Rings:
    def __init__(self, nz, x, z, ga, gb, sems, gi=None, isems=None):
        self.nz, self.x, self.z, self.half = nz, x, z, nz // 2
        self.ga, self.gb, self.gi = ga, gb, gi
        self.sa, self.sb, self.ra_x, self.rb_z, self.ra_z, self.rb_x = sems
        if gi is not None:
            self.si, self.ri_x, self.ri_z = isems
        self.rows_b = gb.shape[1]
        self.low = self.rows_b // 2
        self.right, self.left = self.dev(1, 0), self.dev(-1, 0)
        self.ends = {1: self.dev(0, 1), -1: self.dev(0, -1)}

    def slot(self, dx, dz):
        return lax.rem(self.x + dx + NX, NX) * self.nz + lax.rem(self.z + dz + self.nz, self.nz)

    def dev(self, dx, dz):
        return {"seq": self.slot(dx, dz)}

    def last(self, way):
        return self.half if way > 0 else self.half - 1

    def a_move(self, dx, dist, way):
        at = self.slot(dx, -way * dist)
        lane = 0 if way > 0 else 1
        push(self.ga.at[at], self.ga.at[at], self.sa, self.ra_z.at[dx, lane, dist], self.ends[way])
        if self.gi is not None:
            push(self.gi.at[at], self.gi.at[at], self.si, self.ri_z.at[dx, lane, dist], self.ends[way])

    def a_wait(self, dx, dist, way):
        at = self.slot(dx, -way * dist)
        lane = 0 if way > 0 else 1
        arrived(self.ga.at[at], self.ra_z.at[dx, lane, dist - 1])
        if self.gi is not None:
            arrived(self.gi.at[at], self.ri_z.at[dx, lane, dist - 1])

    def b_move(self, dist, way):
        at = self.slot(0, -way * dist)
        push(self.gb.at[at], self.gb.at[at], self.sb, self.rb_z.at[0 if way > 0 else 1, dist], self.ends[way])

    def b_side(self, dist, way):
        at = self.slot(0, -way * dist)
        lane = 0 if way > 0 else 1
        push(self.gb.at[at], self.gb.at[at], self.sb, self.rb_x.at[0, lane, dist], self.right)
        push(self.gb.at[at], self.gb.at[at], self.sb, self.rb_x.at[1, lane, dist], self.left)

    def halves(self, at):
        return self.gb.at[at, pl.ds(0, self.low)], self.gb.at[at, pl.ds(self.low, self.rows_b - self.low)]

    def b_relay(self, dist, way):
        lane = 0 if way > 0 else 1
        at = self.slot(-1, -way * dist)
        arrived(self.gb.at[at], self.rb_x.at[0, lane, dist])
        part = self.halves(at)[0]
        push(part, part, self.sb, self.rb_x.at[2, lane, dist], self.right)
        at = self.slot(1, -way * dist)
        arrived(self.gb.at[at], self.rb_x.at[1, lane, dist])
        part = self.halves(at)[1]
        push(part, part, self.sb, self.rb_x.at[3, lane, dist], self.left)

    def begin(self):
        me = self.slot(0, 0)
        for dx in (1, 3, 2):
            push(self.ga.at[me], self.ga.at[me], self.sa, self.ra_x.at[dx], self.dev(dx, 0))
            if self.gi is not None:
                push(self.gi.at[me], self.gi.at[me], self.si, self.ri_x.at[dx], self.dev(dx, 0))
        self.b_move(0, 1)
        self.b_move(0, -1)
        self.b_side(0, 1)
        self.a_move(0, 0, 1)
        self.a_move(0, 0, -1)

    def spread(self):
        for dx in (1, 3, 2):
            arrived(self.ga.at[self.slot(dx, 0)], self.ra_x.at[NX - dx])
            if self.gi is not None:
                arrived(self.gi.at[self.slot(dx, 0)], self.ri_x.at[NX - dx])
            self.a_move(dx, 0, 1)
            self.a_move(dx, 0, -1)

    def step(self, k):
        for way in (1, -1):
            if k <= self.last(way):
                arrived(self.gb.at[self.slot(0, -way * k)], self.rb_z.at[0 if way > 0 else 1, k - 1])
                if k < self.last(way):
                    self.b_move(k, way)
                self.b_side(k, way)
        for dx in (0, 1, 3, 2):
            for way in (1, -1):
                if k <= self.last(way):
                    self.a_wait(dx, k, way)
                    if k < self.last(way):
                        self.a_move(dx, k, way)
        for way in (1, -1):
            if k - 1 > 0 or way > 0:
                self.b_relay(k - 1, way)

    def finish(self):
        self.b_relay(self.half, 1)
        for dist in range(self.half + 1):
            for way in (1, -1):
                if way < 0 and (dist == 0 or dist == self.half):
                    continue
                lane = 0 if way > 0 else 1
                low, high = self.halves(self.slot(2, -way * dist))
                arrived(low, self.rb_x.at[2, lane, dist])
                arrived(high, self.rb_x.at[3, lane, dist])

    def drain(self):
        count = NX * self.nz
        arrived(self.ga.at[pl.ds(0, count - 1)], self.sa)
        arrived(self.gb.at[pl.ds(0, count - 1)], self.sb)
        if self.gi is not None:
            arrived(self.gi.at[pl.ds(0, count - 1)], self.si)


def kernel(nz, q_ref, sk_ref, sv_ref, pk_ref, pv_ref, block_ref, row_ref, w_ref, out_ref,
           ga, gb, gi, wa, wb, wt, ks, vs, scores, att, inv_v, inv_s, sem, *sems):
    ring_sems, id_sems, w_sems = sems[0:6], sems[6:9], sems[9:15]
    sp, rp, sg, rg_y, rg_c = sems[15:]
    half = nz // 2
    count = NX * nz
    first = count // 2
    tokens = q_ref.shape[0]
    heads = q_ref.shape[1] // HD
    cols = w_ref.shape[0]
    me, t = lax.axis_index("seq"), lax.axis_index("tp")
    x, z, y, c = me // nz, lax.rem(me, nz), t // 2, lax.rem(t, 2)

    other_half = z // half
    w_slot = lax.rem(y + 1, NX) * nz + lax.rem(half * other_half + 2 * lax.rem(z, half) + c - nz // 4 + nz, nz)
    w_to = {"seq": w_slot, "tp": 2 * x + other_half}
    v = lax.rem(z + nz // 4 - half * c + nz, nz)
    w_from = {"seq": y * nz + half * c + v // 2, "tp": 2 * lax.rem(x + NX - 1, NX) + lax.rem(v, 2)}
    partner = {"tp": 2 * y + 1 - c}

    def column(dy):
        return 2 * lax.rem(y + dy, NY) + c

    kv = Rings(nz, x, z, ga, gb, ring_sems, gi, id_sems)
    wr = Rings(nz, x, z, wa, wb, w_sems)

    barrier = pltpu.get_barrier_semaphore()
    peers = [kv.dev(1, 0), kv.dev(-1, 0), kv.dev(2, 0), kv.dev(0, 1), kv.dev(0, -1), w_to, w_from, partner]
    peers = peers + [{"tp": column(dy)} for dy in range(1, NY)]
    for peer in peers:
        pl.semaphore_signal(barrier, inc=1, device_id=peer, device_id_type=MESH)

    ga[me] = pk_ref[:PART, :]
    gb[me, :HD, :] = pv_ref[...]
    gb[me, HD:, :] = pk_ref[PART:, :]
    gi[me] = jnp.full((1, HD), block_ref[0], jnp.int32)
    for h in range(heads):
        wt[h * cols:(h + 1) * cols, :] = w_ref[:, h * HD:(h + 1) * HD]

    row = jnp.broadcast_to(row_ref[...].astype(jnp.float32), (tokens, tokens))
    col = row.T
    mine = lax.broadcasted_iota(jnp.int32, (tokens, tokens), 0)
    other = lax.broadcasted_iota(jnp.int32, (tokens, tokens), 1)
    same = jnp.where(row == col, 1.0, 0.0)
    offset = jnp.sum(jnp.where(other < mine, same, 0.0), axis=1, keepdims=True)
    lane = lax.broadcasted_iota(jnp.int32, (1, HD), 1)
    low = jnp.float32(-1e30)
    main = first * HD
    total = main + HD + tokens
    ks[main + HD:, :] = sk_ref[...]
    vs[main + HD:, :] = sv_ref[...]

    pl.semaphore_wait(barrier, len(peers))
    kv.begin()
    push(wt.at[pl.ds(0, PART)], wa.at[w_slot], sp, rp.at[0], w_to)
    push(wt.at[pl.ds(PART, wt.shape[0] - PART)], wb.at[w_slot], sp, rp.at[1], w_to)
    kv.spread()
    ahead = max(half - LEAD, 1)
    for k in range(1, half + 1):
        kv.step(k)
        if k == ahead:
            arrived(wa.at[me], rp.at[0])
            arrived(wb.at[me], rp.at[1])
            wr.begin()
            wr.spread()
        elif k > ahead:
            wr.step(k - ahead)
    kv.finish()

    which = lax.broadcasted_iota(jnp.int32, (count, 1, HD), 0)
    inv_v[...] = jnp.max(jnp.where(gi[...] == lane[None], which, 0), axis=0)
    copy = pltpu.make_async_copy(inv_v, inv_s, sem)
    copy.start()
    copy.wait()

    def fetch(to, at):
        ks[pl.ds(to, PART), :] = ga[at]
        ks[pl.ds(to + PART, HD - PART), :] = gb[at, HD:, :]
        vs[pl.ds(to, HD), :] = gb[at, :HD, :]

    def fill(i, _):
        fetch(pl.multiple_of(i * HD, HD), inv_s[0, first + i])
        return 0

    lax.fori_loop(0, first, fill, 0)
    fetch(main, inv_s[0, 0])

    edge = lane.astype(jnp.float32) > offset
    own = (same > 0.5) & (other <= mine)
    sink = lane < SINKS
    gain = jnp.float32(LOG2E / math.sqrt(HD))
    tile = 512
    bounds = [(s, min(tile, total - s)) for s in range(0, main, tile)] + [(main, total - main)]

    def ag_send(h):
        at = t * heads + h
        for dy in (1, 3, 2):
            push(att.at[at], att.at[at], sg, rg_y.at[dy, h], {"tp": column(dy)})
        push(att.at[at], att.at[at], sg, rg_c.at[0, h], partner)

    def ag_relay(h):
        for dy in (1, 3, 2):
            at = column(dy) * heads + h
            arrived(att.at[at], rg_y.at[NY - dy, h])
            push(att.at[at], att.at[at], sg, rg_c.at[dy, h], partner)

    ticks = iter(range(half - ahead + 1, half + 1))

    def tick():
        k = next(ticks, None)
        if k is not None:
            wr.step(k)

    for h in range(heads):
        q = q_ref[:, h * HD:(h + 1) * HD]
        top = jnp.full((tokens, HD), low, jnp.float32)
        for start, size in bounds:
            s = nt(q, ks[start:start + size, :])
            parts = [s[:, j:j + HD] for j in range(0, size, HD)]
            if start == 0:
                parts[0] = jnp.where(edge, parts[0], low)
            if start == main:
                parts[0] = jnp.where(sink, parts[0], low)
                for j in range(1, len(parts)):
                    parts[j] = jnp.where(own[:, (j - 1) * HD:j * HD], parts[j], low)
            for j, part in enumerate(parts):
                scores[:, start + j * HD:start + (j + 1) * HD] = part
                top = jnp.maximum(top, part)
        top = jnp.max(top, axis=1, keepdims=True)
        tick()
        sums = jnp.zeros((tokens, HD), jnp.float32)
        acc = jnp.zeros((tokens, HD), jnp.float32)
        for start, size in bounds:
            w = jnp.exp2((scores[:, start:start + size] - top) * gain)
            for j in range(0, size, HD):
                sums = sums + w[:, j:j + HD]
            acc = acc + jnp.dot(w.astype(jnp.bfloat16), vs[start:start + size, :],
                                preferred_element_type=jnp.float32)
        att[t * heads + h] = (acc / jnp.sum(sums, axis=1, keepdims=True)).astype(jnp.bfloat16)
        tick()
        ag_send(h)
        if h > 0:
            ag_relay(h - 1)
    ag_relay(heads - 1)
    for k in ticks:
        wr.step(k)
    wr.finish()
    for dy in range(NY):
        for h in range(heads):
            at = (2 * lax.rem(y + dy, NY) + 1 - c) * heads + h
            arrived(att.at[at], rg_c.at[dy, h])

    cut = PART - cols
    result = jnp.zeros((tokens, out_ref.shape[1]), jnp.float32)
    for yy in range(NY):
        for cc in range(2):
            base = ((yy + 1) % NX) * nz
            spots = [base + lax.rem(half * c - nz // 4 + cc + 2 * u + nz, nz) for u in range(half)]
            a = [wa[s] for s in spots]
            b = [wb[s] for s in spots]
            rest = cols - cut
            weight = [
                [p[:cols] for p in a],
                [piece for p, r in zip(a, b) for piece in (p[cols:], r[:rest])],
                [r[rest:rest + cols] for r in b],
                [r[rest + cols:] for r in b],
            ]
            w = jnp.concatenate([jnp.concatenate(pieces, axis=0) for pieces in weight], axis=1)
            from_t = (2 * yy + cc) * heads
            a = jnp.concatenate([att[from_t + h] for h in range(heads)], axis=1)
            result = result + nt(a, w)
    out_ref[...] = result.astype(out_ref.dtype)

    kv.drain()
    wr.drain()
    arrived(wt, sp)
    arrived(att.at[pl.ds(0, (NY - 1) * heads + NY * heads)], sg)


def local(queries, suffix_k, suffix_v, prefix_k, prefix_v, prefix_block, request_ids, out_weight):
    count = lax.axis_size("seq")
    nz = count // NX
    half = nz // 2
    tp = lax.axis_size("tp")
    tokens, width = queries.shape
    heads = width // HD
    cols = out_weight.shape[1]
    total = count // 2 * HD + HD + tokens
    bf = jnp.bfloat16
    dma = pltpu.SemaphoreType.DMA
    ring = [dma, dma, dma((NX,)), dma((2, half)), dma((NX, 2, half)), dma((4, 2, half + 1))]
    whole = pl.BlockSpec(memory_space=pltpu.VMEM)
    return pl.pallas_call(
        functools.partial(kernel, nz),
        out_shape=jax.ShapeDtypeStruct((tokens, cols * count // tp), bf),
        in_specs=[whole] * 5 + [pl.BlockSpec(memory_space=pltpu.SMEM)] + [whole] * 2,
        out_specs=whole,
        scratch_shapes=[
            pltpu.VMEM((count, PART, HD), bf),
            pltpu.VMEM((count, 2 * HD - PART, HD), bf),
            pltpu.VMEM((count, 1, HD), jnp.int32),
            pltpu.VMEM((count, PART, HD), bf),
            pltpu.VMEM((count, heads * cols - PART, HD), bf),
            pltpu.VMEM((heads * cols, HD), bf),
            pltpu.VMEM((total, HD), bf),
            pltpu.VMEM((total, HD), bf),
            pltpu.VMEM((tokens, total), jnp.float32),
            pltpu.VMEM((tp * heads, tokens, HD), bf),
            pltpu.VMEM((1, HD), jnp.int32),
            pltpu.SMEM((1, HD), jnp.int32),
            dma,
        ] + ring + [dma, dma((NX,)), dma((NX, 2, half))] + ring
        + [dma, dma((2,)), dma, dma((NY, heads)), dma((NY, heads))],
        compiler_params=pltpu.CompilerParams(
            collective_id=0, has_side_effects=True, vmem_limit_bytes=56 * 2**20
        ),
        name="block",
    )(queries, suffix_k, suffix_v, prefix_k, prefix_v, prefix_block, request_ids, out_weight.T)


def solution(mesh):
    placed = (
        P("seq", "tp"),
        P("seq", "tp"),
        P("seq", "tp"),
        P("seq", "tp"),
        P("seq", "tp"),
        P("seq"),
        P("seq", None),
        P("tp", "seq"),
    )
    return jax.shard_map(
        local, mesh=mesh, in_specs=placed, out_specs=P("seq", "tp"), check_vma=False
    )
```
